256 devices in a mesh: ctx: 32 (over z, x_lo, core), head: 8 (over x_hi, y).
Axes of the slice: x: 4 (x_hi: 2, x_lo: 2; x = x_hi * 2 + x_lo), y: 4, z: 8, core: 2. Of those that a mesh axis runs over, the one named last changes fastest.
Arguments:
- block_order: int32 [64], replicated, may hold values from 0 to 63, as said below
- queries: bfloat16 [12288, 4096], P('ctx', 'head'), may hold values from -12 to 12
- key_head_matrix: bfloat16 [12288, 1024], P('ctx', 'head'), may hold values from -6 to 6
- value_head_matrix: bfloat16 [12288, 1024], P('ctx', 'head'), may hold values from -6 to 6
- out_weight: bfloat16 [4096, 4096], P('head'), may hold values from -0.125 to 0.125
- filter_taps: float32 [128, 4096], P(None, 'head'), may hold values from -0.5 to 0.5
- skip_gain: float32 [4096], P('head'), may hold values from 0.5 to 1.5
- gate_values: bfloat16 [12288, 4096], P('ctx', 'head'), may hold values from -4 to 4
Outputs:
- mixed_out: bfloat16 [12288, 4096], P('ctx', 'head')
The draws below stay inside these ranges and needn't reach their ends.
Inputs may be any that keep to these rules, and one draw needn't show every extreme that they name: A permutation of the 64 sequence blocks; for every d, block_order[2 d] < 32 and block_order[2 d] + block_order[2 d + 1] = 63.
All inputs are finite; a program needn't handle non-finite values.
Results may differ from the reference program's by a relative error of at most 0.015.
Values may be sent and summed in bfloat16 or wider, within the bound.
No kernel may reach another device: no remote copies, remote signals or barrier semaphores. Data moves between devices by JAX's collectives and lax.ppermute only.
A program may use at most 64 MiB of HBM per device.

```python
import math
import jax
import jax.numpy as jnp
from jax import lax

D = 4096
QUERY_HEADS = 32
KEY_VALUE_HEADS = 8
HEAD_WIDTH = 128
TAPS = 128
QUERY_PER_KV = 4
BLK = 192
NBLK = 64
SEQUENCE_ROWS = 12288
N_HEAD = 8


def draw_block_order(key, part):
    shuffled = jax.random.permutation(key, NBLK // 2).astype(jnp.int32)
    pair_order = jnp.stack([shuffled, NBLK - 1 - shuffled], axis=1)
    return pair_order.reshape(NBLK).astype(jnp.int32)


def query_key_pair(key):
    query_seed = jax.random.fold_in(key, 101)
    key_random_seed = jax.random.fold_in(key, 102)
    query_vals = jnp.clip(3.0 * jax.random.normal(query_seed, (SEQUENCE_ROWS, QUERY_HEADS * HEAD_WIDTH), jnp.float32), -12.0, 12.0)
    key_entries = jnp.clip(jax.random.normal(key_random_seed, (SEQUENCE_ROWS, KEY_VALUE_HEADS * HEAD_WIDTH), jnp.float32), -6.0, 6.0)
    return (query_vals, key_entries)


def draw_queries(key, part):
    return query_key_pair(key)[0].astype(jnp.bfloat16)


def draw_key_head_matrix(key, part):
    return query_key_pair(key)[1].astype(jnp.bfloat16)


def raised(array, stream_key, source, target, blocks, factor):
    def block_of(position):
        return (jnp.arange(array.shape[position]) // (array.shape[position] // blocks)).reshape((-1,) + (1,) * (array.ndim - 1 - position))

    first = jax.random.permutation(stream_key, blocks)[block_of(target)]
    other_side = (block_of(target) + blocks // 2) % blocks
    return jnp.where((block_of(source) == first) | (block_of(source) == other_side), factor * array, array)


def shard_levels(rng, extent, split, least, largest):
    factor_of, own = 1.0, jax.random.fold_in(rng, 6)
    for axis_at, blocks in split:
        draws = jnp.exp(jax.random.uniform(jax.random.fold_in(own, axis_at), (blocks,), jnp.float32, least / len(split), largest / len(split)))
        factor_of = factor_of * jnp.repeat(draws, extent[axis_at] // blocks).reshape([-1 if axis == axis_at else 1 for axis in range(len(extent))])
    return factor_of


def bell_draw(own_key, shape, spread, bound, cuts=(), held_as=jnp.bfloat16):
    values = spread * jax.random.normal(own_key, shape, jnp.float32)
    if cuts:
        values = values * shard_levels(own_key, shape, cuts, -0.22, 0.18)
    return jnp.clip(values, -bound, bound).astype(held_as)


def gaussian_with(key, shape, deviation, bound, shards, heavy, held_as=jnp.bfloat16):
    values = deviation * jax.random.normal(key, shape, jnp.float32)
    if shards:
        values = values * shard_levels(key, shape, shards, -0.22, 0.18)
    return jnp.clip(raised(values, jax.random.fold_in(key, 3), *heavy), -bound, bound).astype(held_as)


def setup_inputs(seed: int = 0) -> dict:
    arg_keys = jax.random.split(jax.random.key(seed), 9)
    block_order = draw_block_order(jax.random.fold_in(arg_keys[8], 71), 0)
    queries = draw_queries(jax.random.fold_in(arg_keys[8], 71), 0)
    key_head_matrix = draw_key_head_matrix(jax.random.fold_in(arg_keys[8], 71), 0)
    value_head_matrix = bell_draw(arg_keys[3], (SEQUENCE_ROWS, KEY_VALUE_HEADS * HEAD_WIDTH), 1.0, 6.0, ((0, 32), (1, 8)))
    out_weight = gaussian_with(arg_keys[4], (QUERY_HEADS * HEAD_WIDTH, D), (QUERY_HEADS * HEAD_WIDTH) ** -0.5, 0.125, ((0, 8),), (0, 1, 8, 2.0))
    filter_taps = bell_draw(arg_keys[5], (TAPS, D), TAPS ** -0.5, 0.5, ((1, 8),), jnp.float32)
    skip_gain = jnp.clip(0.5 + 1.0 * jax.random.uniform(arg_keys[6], (D,), jnp.float32) ** shard_levels(arg_keys[6], (D,), ((0, 8),), -0.2, 0.2), 0.5, 1.5)
    gate_values = bell_draw(arg_keys[7], (SEQUENCE_ROWS, D), 1.0, 4.0, ((0, 32), (1, 8)))
    return {"block_order": block_order, "queries": queries, "key_head_matrix": key_head_matrix, "value_head_matrix": value_head_matrix, "out_weight": out_weight, "filter_taps": filter_taps, "skip_gain": skip_gain, "gate_values": gate_values}


def inverse_order(block_order):
    return jnp.zeros((NBLK,), jnp.int32).at[block_order].set(jnp.arange(NBLK, dtype=jnp.int32))

def reference(block_order, queries, key_head_matrix, value_head_matrix, out_weight, filter_taps, skip_gain, gate_values):
    holder = inverse_order(block_order)

    def restore_sequence_order(array_in):
        return array_in.reshape(NBLK, BLK, -1)[holder].reshape(SEQUENCE_ROWS, -1)

    def to_layout(array_in):
        return array_in.reshape(NBLK, BLK, -1)[block_order].reshape(SEQUENCE_ROWS, -1)
    query_sequence = restore_sequence_order(queries).reshape(SEQUENCE_ROWS, KEY_VALUE_HEADS, QUERY_PER_KV, HEAD_WIDTH)
    key_sequence = restore_sequence_order(key_head_matrix).reshape(SEQUENCE_ROWS, KEY_VALUE_HEADS, HEAD_WIDTH)
    value_sequence = restore_sequence_order(value_head_matrix).reshape(SEQUENCE_ROWS, KEY_VALUE_HEADS, HEAD_WIDTH)
    width = math.gcd(SEQUENCE_ROWS, 512)
    scaling = 1.0 / math.sqrt(HEAD_WIDTH)
    outputs = []
    for number in range(SEQUENCE_ROWS // width):
        finish = (number + 1) * width
        query_part = jnp.moveaxis(query_sequence[number * width:finish], 1, 0)
        key_part = jnp.moveaxis(key_sequence[:finish], 1, 0)
        value_part = jnp.moveaxis(value_sequence[:finish], 1, 0)
        query_place = number * width + jnp.arange(width, dtype=jnp.int32)
        key_place = jnp.arange(finish, dtype=jnp.int32)
        allowed = key_place[None, :] <= query_place[:, None]

        def one_group(operands):
            group_query, group_key, group_value = operands
            scores = jnp.einsum('qgd,kd->gqk', group_query.astype(jnp.float32), group_key.astype(jnp.float32)) * scaling
            scores = jnp.where(allowed[None], scores, -jnp.inf)
            row_max = lax.optimization_barrier(jnp.max(scores, axis=-1, keepdims=True))
            weight = jnp.where(allowed[None], jnp.exp(scores - row_max), 0.0)
            row_total = lax.optimization_barrier(jnp.sum(weight, axis=-1))
            rounded = lax.optimization_barrier(weight.astype(jnp.bfloat16)).astype(jnp.float32)
            summed = jnp.einsum('gqk,kd->qgd', rounded, group_value.astype(jnp.float32))
            return summed / jnp.transpose(row_total)[:, :, None]
        attended = lax.map(one_group, (query_part, key_part, value_part))
        outputs.append(jnp.moveaxis(attended, 0, 1).reshape(width, QUERY_HEADS * HEAD_WIDTH))
    attended = jnp.concatenate(outputs, axis=0).astype(jnp.bfloat16)
    share_cols = QUERY_HEADS * HEAD_WIDTH // N_HEAD
    projected = jnp.zeros((SEQUENCE_ROWS, D), jnp.float32)
    for group in range(N_HEAD):
        partial_value = jnp.dot(attended[:, group * share_cols:(group + 1) * share_cols], out_weight[group * share_cols:(group + 1) * share_cols], preferred_element_type=jnp.float32)
        projected = projected + lax.optimization_barrier(partial_value.astype(jnp.bfloat16)).astype(jnp.float32)
    projected = projected.astype(jnp.bfloat16)
    source = projected.astype(jnp.float32)
    padded = jnp.concatenate([jnp.zeros((TAPS - 1, D), jnp.float32), source], axis=0)

    def add_tap(tap_index, running):
        begin = (TAPS - 1 - tap_index).astype(jnp.int32)
        return running + filter_taps[tap_index][None, :] * lax.dynamic_slice_in_dim(padded, begin, SEQUENCE_ROWS, 0)
    filtered = lax.fori_loop(0, TAPS, add_tap, jnp.zeros((SEQUENCE_ROWS, D), jnp.float32))
    gate_seq = restore_sequence_order(gate_values).astype(jnp.float32)
    mixed_rows = gate_seq * (filtered + skip_gain[None, :] * source)
    return to_layout(mixed_rows.astype(jnp.bfloat16))
```

```python
import functools
import math

import jax
import jax.numpy as jnp
from jax import lax
from jax.experimental import pallas as pl
from jax.experimental.pallas import tpu as pltpu
from jax.sharding import PartitionSpec as P

HEAD_WIDTH = 128
QUERY_PER_KV = 4
GROUP = 4
LOW = -1e30
LOG2_E = 1.4426950408889634


def lookup(table_values, index_values):
    matches = jnp.arange(table_values.shape[0], dtype=jnp.int32)[None, :] == index_values[:, None]
    return jnp.sum(jnp.where(matches, table_values[None, :], 0), axis=1)


def attention_kernel(
    block_rows, holder, own, q_ref, kv_ref, o_ref, qs_ref, m_ref, acc_ref
):
    scale = LOG2_E / math.sqrt(HEAD_WIDTH)
    for s in range(2):
        for h in range(QUERY_PER_KV):
            q = q_ref[
                s * block_rows : (s + 1) * block_rows, h * HEAD_WIDTH : (h + 1) * HEAD_WIDTH
            ].astype(jnp.float32)
            q = q * scale
            high = q.astype(jnp.bfloat16)
            rest = (q - high.astype(jnp.float32)).astype(jnp.bfloat16)
            qs_ref[s, h, :, :HEAD_WIDTH] = high
            qs_ref[s, h, :, HEAD_WIDTH:] = rest
    m_ref[...] = jnp.full_like(m_ref, LOW)
    acc_ref[...] = jnp.zeros_like(acc_ref)
    keys = GROUP * block_rows

    def step(s, group, masked):
        pieces = []
        for j in range(GROUP):
            start = pl.multiple_of(holder[group * GROUP + j] * block_rows, block_rows)
            pieces.append(kv_ref[pl.ds(start, block_rows), :])
        kv = jnp.concatenate(pieces, axis=0)
        k = kv[:, :HEAD_WIDTH]
        k2 = jnp.concatenate([k, k], axis=1)
        v1 = jnp.concatenate([kv[:, HEAD_WIDTH:], jnp.ones_like(k)], axis=1)
        if masked:
            key_at = group * keys + lax.broadcasted_iota(jnp.int32, (block_rows, keys), 1)
            query_at = own[s] * block_rows + lax.broadcasted_iota(
                jnp.int32, (block_rows, keys), 0
            )
            allowed = key_at <= query_at
        for h in range(QUERY_PER_KV):
            scores = lax.dot_general(
                qs_ref[s, h], k2, (((1,), (1,)), ((), ())), preferred_element_type=jnp.float32
            )
            if masked:
                scores = jnp.where(allowed, scores, LOW)
            old = m_ref[s, h]
            newest = jnp.maximum(old, jnp.max(scores, axis=1, keepdims=True))
            weight = jnp.exp2(scores - jnp.concatenate([newest] * (keys // HEAD_WIDTH), axis=1))
            factor = jnp.exp2(old - newest)
            m_ref[s, h] = newest
            acc_ref[s, h] = acc_ref[s, h] * jnp.concatenate([factor, factor], axis=1) + jnp.dot(
                weight.astype(jnp.bfloat16), v1, preferred_element_type=jnp.float32
            )

    for s in range(2):
        last = own[s] // GROUP

        def plain(group, unused):
            step(s, group, False)
            return unused

        lax.fori_loop(0, last, plain, 0)
        step(s, last, True)
    for s in range(2):
        for h in range(QUERY_PER_KV):
            o_ref[
                s * block_rows : (s + 1) * block_rows, h * HEAD_WIDTH : (h + 1) * HEAD_WIDTH
            ] = (acc_ref[s, h, :, :HEAD_WIDTH] / acc_ref[s, h, :, HEAD_WIDTH:]).astype(
                jnp.bfloat16
            )


def attention(holder, own, queries, kv):
    rows = queries.shape[0]
    block_rows = rows // 2
    vmem = pl.BlockSpec(memory_space=pltpu.VMEM)
    return pl.pallas_call(
        functools.partial(attention_kernel, block_rows),
        out_shape=jax.ShapeDtypeStruct(queries.shape, jnp.bfloat16),
        grid_spec=pltpu.PrefetchScalarGridSpec(
            num_scalar_prefetch=2,
            grid=(),
            in_specs=[vmem, vmem],
            out_specs=vmem,
            scratch_shapes=[
                pltpu.VMEM((2, QUERY_PER_KV, block_rows, 2 * HEAD_WIDTH), jnp.bfloat16),
                pltpu.VMEM((2, QUERY_PER_KV, block_rows, HEAD_WIDTH), jnp.float32),
                pltpu.VMEM((2, QUERY_PER_KV, block_rows, 2 * HEAD_WIDTH), jnp.float32),
            ],
        ),
        name="attention",
    )(holder, own, queries, kv)


def inside_kernel(x_ref, taps_ref, o_ref, ext_ref):
    rows = x_ref.shape[1]
    taps = taps_ref.shape[0]
    ext_ref[:taps, :] = jnp.zeros((taps, ext_ref.shape[1]), jnp.float32)
    ext_ref[taps:, :] = x_ref[0].astype(jnp.float32)
    half = rows // 2
    for part in range(2):
        total = jnp.zeros((half, ext_ref.shape[1]), jnp.float32)
        for j in range(8):
            base = 8 + half * part - j
            piece = ext_ref[pl.ds(base, half + taps - 8), :]
            for k in range(taps // 8):
                tap = taps_ref[pl.ds(8 * k + j, 1), :]
                skip = max(0, 8 * k - half * part) // 8 * 8
                if skip >= half:
                    continue
                low = taps - 8 - 8 * k + skip
                term = tap * piece[low : low + half - skip, :]
                if skip:
                    total = jnp.concatenate([total[:skip], total[skip:] + term], axis=0)
                else:
                    total = total + term
        o_ref[0, half * part : half * (part + 1), :] = total


def inside_filter(x, taps):
    blocks, rows, channels = x.shape
    return pl.pallas_call(
        inside_kernel,
        out_shape=jax.ShapeDtypeStruct(x.shape, jnp.float32),
        grid=(blocks, channels // 128),
        in_specs=[
            pl.BlockSpec((1, rows, 128), lambda s, c: (s, 0, c)),
            pl.BlockSpec((taps.shape[0], 128), lambda s, c: (0, c)),
        ],
        out_specs=pl.BlockSpec((1, rows, 128), lambda s, c: (s, 0, c)),
        scratch_shapes=[pltpu.VMEM((rows + taps.shape[0], 128), jnp.float32)],
        name="inside",
    )(x, taps)


def finish_kernel(x_ref, halo_ref, inside_ref, taps_ref, skip_ref, gate_ref, o_ref, ext_ref):
    taps = taps_ref.shape[0]
    ext_ref[:taps, :] = halo_ref[0].astype(jnp.float32)
    ext_ref[taps:, :] = jnp.zeros((taps, ext_ref.shape[1]), jnp.float32)
    half = taps // 2
    added = []
    for part in range(2):
        total = jnp.zeros((half, ext_ref.shape[1]), jnp.float32)
        for j in range(8):
            base = 8 + half * part - j
            piece = ext_ref[pl.ds(base, half + taps - 8), :]
            for k in range(taps // 8):
                tap = taps_ref[pl.ds(8 * k + j, 1), :]
                keep = min(half, 8 * k + 8 - half * part)
                if keep <= 0:
                    continue
                low = taps - 8 - 8 * k
                term = tap * piece[low : low + keep, :]
                if keep < half:
                    total = jnp.concatenate([total[:keep] + term, total[keep:]], axis=0)
                else:
                    total = total + term
        added.append(total)
    rows = x_ref.shape[1]
    added.append(jnp.zeros((rows - taps, ext_ref.shape[1]), jnp.float32))
    filtered = inside_ref[0] + jnp.concatenate(added, axis=0)
    direct = skip_ref[...] * x_ref[0].astype(jnp.float32)
    o_ref[0] = (gate_ref[0].astype(jnp.float32) * (filtered + direct)).astype(jnp.bfloat16)


def finish(x, halo, inside, taps, skip, gate):
    blocks, rows, channels = x.shape
    count = taps.shape[0]
    tile = pl.BlockSpec((1, rows, 128), lambda s, c: (s, 0, c))
    return pl.pallas_call(
        finish_kernel,
        out_shape=jax.ShapeDtypeStruct(x.shape, jnp.bfloat16),
        grid=(blocks, channels // 128),
        in_specs=[
            tile,
            pl.BlockSpec((1, count, 128), lambda s, c: (s, 0, c)),
            tile,
            pl.BlockSpec((count, 128), lambda s, c: (0, c)),
            pl.BlockSpec((1, 128), lambda s, c: (0, c)),
            tile,
        ],
        out_specs=tile,
        scratch_shapes=[pltpu.VMEM((2 * count, 128), jnp.float32)],
        name="finish",
    )(x, halo, inside, taps, skip, gate)


def sum_at_owner(x, axis, dim):
    size = lax.axis_size(axis)
    shape = x.shape
    tiles = x.reshape(*shape[:dim], size, shape[dim] // size, *shape[dim + 1 :])
    tiles = lax.all_to_all(jnp.moveaxis(tiles, dim, 0), axis, 0, 0, tiled=True)
    return jnp.sum(tiles.astype(jnp.float32), axis=0)


def shards(
    block_order,
    queries,
    key_head_matrix,
    value_head_matrix,
    out_weight,
    filter_taps,
    skip_gain,
    gate_values,
):
    local_rows = queries.shape[0]
    block_rows = local_rows // 2
    position = lax.axis_index("ctx")
    own = lookup(block_order, 2 * position + jnp.arange(2, dtype=jnp.int32))
    count = block_order.shape[0]
    places = jnp.arange(count, dtype=jnp.int32)
    holder = jnp.sum(
        jnp.where(block_order[None, :] == places[:, None], places[None, :], 0), axis=1
    )
    kv = lax.all_gather(
        jnp.concatenate([key_head_matrix, value_head_matrix], axis=1), "ctx", axis=0, tiled=True
    )
    attended = attention(holder, own, queries, kv)
    partials = jnp.dot(attended, out_weight, preferred_element_type=jnp.float32)
    projected = sum_at_owner(partials.astype(jnp.bfloat16), "head", 1).astype(jnp.bfloat16)
    channels = projected.shape[1]
    taps = filter_taps.shape[0]
    blocks_here = projected.reshape(2, block_rows, channels)
    tail_rows = blocks_here[:, block_rows - taps :, :]
    piece = lax.all_gather(tail_rows, "ctx", axis=0, tiled=True)
    inside = inside_filter(blocks_here, filter_taps)
    source = lookup(holder, jnp.maximum(own - 1, 0))
    halo = jnp.where((own > 0)[:, None, None], jnp.take(piece, source, axis=0), 0)
    out = finish(
        blocks_here,
        halo,
        inside,
        filter_taps,
        skip_gain[None, :],
        gate_values.reshape(2, block_rows, channels),
    )
    return out.reshape(local_rows, channels)


def solution(mesh):
    return jax.shard_map(
        shards,
        mesh=mesh,
        in_specs=(
            P(),
            P("ctx", "head"),
            P("ctx", "head"),
            P("ctx", "head"),
            P("head", None),
            P(None, "head"),
            P("head"),
            P("ctx", "head"),
        ),
        out_specs=P("ctx", "head"),
        check_vma=False,
    )
```

```python
import functools
import math

import jax
import jax.numpy as jnp
from jax import lax
from jax.experimental import pallas as pl
from jax.experimental.pallas import tpu as pltpu
from jax.sharding import PartitionSpec as P

HEAD_WIDTH = 128
QUERY_PER_KV = 4
GROUP = 4
LOW = -1e30
LOG2_E = 1.4426950408889634
RING = 8
COLUMN = 4
SLOT_Z = (0, 0, -1, -1, -2, -2, -3, -3, 1, 1, 2, 2, 3, 3, 4, 4)
TAIL_Z = (0, -1, -2, -3, 1, 2, 3, 4)
VMEM = pl.BlockSpec(memory_space=pltpu.VMEM)
ANY = pl.BlockSpec(memory_space=pl.ANY)
SMEM = pl.BlockSpec(memory_space=pltpu.SMEM)


def lookup(table_values, index_values):
    matches = jnp.arange(table_values.shape[0], dtype=jnp.int32)[None, :] == index_values[:, None]
    return jnp.sum(jnp.where(matches, table_values[None, :], 0), axis=1)


def along_z(x, distance):
    pairs = [
        (i, (i // COLUMN + distance) % RING * COLUMN + i % COLUMN) for i in range(RING * COLUMN)
    ]
    return lax.ppermute(x, "ctx", pairs)


def across(x, bits):
    return lax.ppermute(x, "ctx", [(i, i ^ bits) for i in range(RING * COLUMN)])


def head_target(index, k):
    return (index // 4 ^ k // 4) * 4 + (index + k) % 4


def estimate(flops, moved, exps=0):
    return pl.CostEstimate(flops=flops, bytes_accessed=moved, transcendentals=exps)


def prepare_kernel(own_ref, other_ref, low_ref, high_ref):
    scale = LOG2_E / math.sqrt(HEAD_WIDTH)
    rows = own_ref.shape[0] // 2
    for i, q_ref in enumerate((own_ref, other_ref)):
        for s, out in enumerate((low_ref, high_ref)):
            for h in range(QUERY_PER_KV):
                q = q_ref[
                    s * rows : (s + 1) * rows, h * HEAD_WIDTH : (h + 1) * HEAD_WIDTH
                ].astype(jnp.float32)
                q = q * scale
                high = q.astype(jnp.bfloat16)
                rest = (q - high.astype(jnp.float32)).astype(jnp.bfloat16)
                out[i, h, :, :HEAD_WIDTH] = high
                out[i, h, :, HEAD_WIDTH:] = rest


def prepare(own, other):
    rows = own.shape[0] // 2
    shape = jax.ShapeDtypeStruct((2, QUERY_PER_KV, rows, 2 * HEAD_WIDTH), jnp.bfloat16)
    return pl.pallas_call(
        prepare_kernel,
        out_shape=(shape, shape),
        in_specs=[VMEM, VMEM],
        out_specs=(VMEM, VMEM),
        cost_estimate=estimate(10**6, 2 * 10**6),
        name="prepare",
    )(own, other)


def operands(pieces):
    kv = jnp.concatenate(pieces, axis=0)
    k = kv[:, :HEAD_WIDTH]
    k2 = jnp.concatenate([k, k], axis=1)
    v1 = jnp.concatenate([kv[:, HEAD_WIDTH:], jnp.ones_like(k)], axis=1)
    return k2, v1


def attend(i, pair, q_ref, m_ref, acc_ref, limit=None):
    k2, v1 = pair
    keys = k2.shape[0]
    rows = q_ref.shape[2]
    if limit is not None:
        key_at = lax.broadcasted_iota(jnp.int32, (rows, keys), 1)
        allowed = key_at <= limit(lax.broadcasted_iota(jnp.int32, (rows, keys), 0))
    for h in range(QUERY_PER_KV):
        scores = lax.dot_general(
            q_ref[i, h], k2, (((1,), (1,)), ((), ())), preferred_element_type=jnp.float32
        )
        if limit is not None:
            scores = jnp.where(allowed, scores, LOW)
        old = m_ref[i, h]
        newest = jnp.maximum(old, jnp.max(scores, axis=1, keepdims=True))
        weight = jnp.exp2(scores - jnp.concatenate([newest] * (keys // HEAD_WIDTH), axis=1))
        if limit is not None:
            weight = jnp.where(allowed, weight, 0.0)
        factor = jnp.exp2(old - newest)
        m_ref[i, h] = newest
        acc_ref[i, h] = acc_ref[i, h] * jnp.concatenate([factor, factor], axis=1) + jnp.dot(
            weight.astype(jnp.bfloat16), v1, preferred_element_type=jnp.float32
        )


def low_blocks(refs, rows):
    pieces = []
    for ref in refs:
        for start in range(0, ref.shape[0], 2 * rows):
            pieces.append(ref[start : start + rows, :])
    return pieces


def fold_kernel(first, count, *refs):
    q_ref, arrays = refs[0], refs[1 : 1 + count]
    m_ref, acc_ref = refs[-2:]
    rows = q_ref.shape[2]
    if first:
        m_ref[...] = jnp.full_like(m_ref, LOW)
        acc_ref[...] = jnp.zeros_like(acc_ref)
    else:
        m_ref[...] = refs[1 + count][...]
        acc_ref[...] = refs[2 + count][...]

    def one(i, unused):
        attend(i, operands(low_blocks(arrays, rows)), q_ref, m_ref, acc_ref)
        return unused

    lax.fori_loop(0, 2, one, 0)


def state_shapes(rows):
    return (
        jax.ShapeDtypeStruct((2, QUERY_PER_KV, rows, HEAD_WIDTH), jnp.float32),
        jax.ShapeDtypeStruct((2, QUERY_PER_KV, rows, 2 * HEAD_WIDTH), jnp.float32),
    )


def fold(q_high, arrays, state):
    rows = q_high.shape[2]
    keys = sum(a.shape[0] // 2 for a in arrays)
    first = state is None
    args = (q_high, *arrays) + (() if first else state)
    count = 1 + len(arrays)
    return pl.pallas_call(
        functools.partial(fold_kernel, first, len(arrays)),
        out_shape=state_shapes(rows),
        in_specs=[VMEM] * len(args),
        out_specs=(VMEM, VMEM),
        input_output_aliases={} if first else {count: 0, count + 1: 1},
        cost_estimate=estimate(8 * rows * keys * 1024, 6 * 10**6, 8 * rows * keys),
        name="fold",
    )(*args)


def side_kernel(side, info, q_ref, *refs):
    arrays = refs[:10]
    if side:
        m_in, acc_in = refs[10:12]
        refs = refs[12:]
    else:
        refs = refs[10:]
    own_out, other_out, kv_ref, m_ref, acc_ref, list_ref, sem = refs
    rows = q_ref.shape[2]
    slots = 2 * RING
    copies = []
    slot = 0
    for ref in arrays:
        for start in range(side * rows, ref.shape[0], 2 * rows):
            copies.append(
                pltpu.make_async_copy(
                    ref.at[pl.ds(start, rows), :], kv_ref.at[slot], sem.at[slot]
                )
            )
            slot += 1
    late = []
    if side:
        for ref in arrays[-2:]:
            copies.append(
                pltpu.make_async_copy(ref.at[pl.ds(0, rows), :], kv_ref.at[slot], sem.at[slot])
            )
            late.append(slot)
            slot += 1
    for copy in copies:
        copy.start()
    if side:
        m_ref[...] = m_in[...]
        acc_ref[...] = acc_in[...]
    else:
        m_ref[...] = jnp.full_like(m_ref, LOW)
        acc_ref[...] = jnp.zeros_like(acc_ref)
    counts = []
    for i in range(2):
        number = jnp.int32(0)
        mine = info[slots + i]
        for p in range(slots + 8):
            list_ref[i, p] = 0
        for p in range(slots):
            list_ref[i, number] = p
            chosen = info[p] > mine if side else info[p] < mine
            number = number + chosen.astype(jnp.int32)
        list_ref[i, number] = 0
        counts.append(number)
    for copy in copies:
        copy.wait()
    if late:

        def extra(i, unused):
            attend(i, operands([kv_ref[p] for p in late]), q_ref, m_ref, acc_ref)
            return unused

        lax.fori_loop(0, 2, extra, 0)
    for i in range(2):

        def gathered(group):
            return operands([kv_ref[list_ref[i, group * GROUP + j]] for j in range(GROUP)])

        def plain(group, unused):
            attend(i, gathered(group), q_ref, m_ref, acc_ref)
            return unused

        whole = counts[i] // GROUP
        lax.fori_loop(0, whole, plain, 0)
        left = counts[i] - whole * GROUP

        def rest():
            edge = left * rows

            def limit(row):
                return edge + row if i == 0 else edge - 1

            attend(i, gathered(whole), q_ref, m_ref, acc_ref, limit)

        if i == 0:
            rest()
        else:
            pl.when(left > 0)(rest)
    for i, out in enumerate((own_out, other_out)):
        for h in range(QUERY_PER_KV):
            total = jnp.maximum(acc_ref[i, h, :, HEAD_WIDTH:], 1e-30)
            out[h, :, :HEAD_WIDTH] = acc_ref[i, h, :, :HEAD_WIDTH] / total
            out[h, :, HEAD_WIDTH:] = m_ref[i, h] + jnp.log2(total)


def one_side(side, info, q, arrays, state):
    rows = q.shape[2]
    shape = jax.ShapeDtypeStruct((QUERY_PER_KV, rows, 2 * HEAD_WIDTH), jnp.float32)
    slots = 2 * RING + 2 * side
    return pl.pallas_call(
        functools.partial(side_kernel, side),
        out_shape=(shape, shape),
        in_specs=[SMEM, VMEM] + [ANY] * len(arrays) + [VMEM] * len(state),
        out_specs=(VMEM, VMEM),
        scratch_shapes=[
            pltpu.VMEM((slots, rows, 2 * HEAD_WIDTH), jnp.bfloat16),
            *(pltpu.VMEM(s.shape, s.dtype) for s in state_shapes(rows)),
            pltpu.SMEM((2, 2 * RING + 8), jnp.int32),
            pltpu.SemaphoreType.DMA((slots,)),
        ],
        cost_estimate=estimate(8 * rows * rows * 8 * 1024, 8 * 10**6, 64 * rows * rows),
        name="high_side" if side else "low_side",
    )(info, q, *arrays, *state)


def project_kernel(target, own_ref, other_ref, w_ref, *outs):
    parts = []
    for h in range(QUERY_PER_KV):
        one, two = own_ref[h, :, HEAD_WIDTH:], other_ref[h, :, HEAD_WIDTH:]
        top = jnp.maximum(one, two)
        one, two = jnp.exp2(one - top), jnp.exp2(two - top)
        mixed = own_ref[h, :, :HEAD_WIDTH] * one + other_ref[h, :, :HEAD_WIDTH] * two
        parts.append((mixed / (one + two)).astype(jnp.bfloat16))
    attended = jnp.concatenate(parts, axis=1)
    width = outs[0].shape[1]
    for k, out in enumerate(outs):
        start = pl.multiple_of(target[k] * width, width)
        out[...] = jnp.dot(
            attended, w_ref[:, pl.ds(start, width)], preferred_element_type=jnp.float32
        ).astype(jnp.bfloat16)


def project(target, own, other, weight):
    rows = own.shape[1]
    count = target.shape[0]
    width = weight.shape[1] // count
    shape = jax.ShapeDtypeStruct((rows, width), jnp.bfloat16)
    return pl.pallas_call(
        project_kernel,
        out_shape=(shape,) * count,
        in_specs=[SMEM, VMEM, VMEM, VMEM],
        out_specs=(VMEM,) * count,
        cost_estimate=estimate(2 * rows * weight.shape[0] * weight.shape[1], 6 * 10**6),
        name="project",
    )(target, own, other, weight)


def total_kernel(*refs):
    parts, (out_ref, tail_ref) = refs[:-2], refs[-2:]
    total = parts[0][...].astype(jnp.float32)
    for part in parts[1:]:
        total = total + part[...].astype(jnp.float32)
    total = total.astype(jnp.bfloat16)
    out_ref[...] = total
    tail_ref[...] = total[total.shape[0] - tail_ref.shape[0] :, :]


def total_of(parts, taps):
    rows, width = parts[0].shape
    return pl.pallas_call(
        total_kernel,
        out_shape=(
            jax.ShapeDtypeStruct((rows, width), jnp.bfloat16),
            jax.ShapeDtypeStruct((taps, width), jnp.bfloat16),
        ),
        in_specs=[VMEM] * len(parts),
        out_specs=(VMEM, VMEM),
        cost_estimate=estimate(10**6, 2 * 10**6),
        name="total",
    )(*parts)


def inside_kernel(x_ref, taps_ref, o_ref, ext_ref):
    rows = x_ref.shape[0]
    taps = taps_ref.shape[0]
    ext_ref[:taps, :] = jnp.zeros((taps, ext_ref.shape[1]), jnp.float32)
    ext_ref[taps:, :] = x_ref[...].astype(jnp.float32)
    half = rows // 2
    for part in range(2):
        total = jnp.zeros((half, ext_ref.shape[1]), jnp.float32)
        for j in range(8):
            base = 8 + half * part - j
            piece = ext_ref[pl.ds(base, half + taps - 8), :]
            for k in range(taps // 8):
                tap = taps_ref[pl.ds(8 * k + j, 1), :]
                skip = max(0, 8 * k - half * part) // 8 * 8
                if skip >= half:
                    continue
                low = taps - 8 - 8 * k + skip
                term = tap * piece[low : low + half - skip, :]
                if skip:
                    total = jnp.concatenate([total[:skip], total[skip:] + term], axis=0)
                else:
                    total = total + term
        o_ref[half * part : half * (part + 1), :] = total


def inside_filter(x, taps):
    rows, channels = x.shape
    return pl.pallas_call(
        inside_kernel,
        out_shape=jax.ShapeDtypeStruct(x.shape, jnp.float32),
        grid=(channels // 128,),
        in_specs=[
            pl.BlockSpec((rows, 128), lambda c: (0, c)),
            pl.BlockSpec((taps.shape[0], 128), lambda c: (0, c)),
        ],
        out_specs=pl.BlockSpec((rows, 128), lambda c: (0, c)),
        scratch_shapes=[pltpu.VMEM((rows + taps.shape[0], 128), jnp.float32)],
        cost_estimate=estimate(2 * rows * channels * 128, 10**6),
        name="inside",
    )(x, taps)


def choose_kernel(slot, *refs):
    sources, outs, sem = refs[: len(TAIL_Z)], refs[len(TAIL_Z) : -1], refs[-1]
    for k, out in enumerate(outs):
        for n, source in enumerate(sources):

            @pl.when(slot[k] == n)
            def _():
                pltpu.make_async_copy(source, out, sem.at[k]).start()

    for k, out in enumerate(outs):
        pltpu.make_async_copy(sources[0], out, sem.at[k]).wait()


def choose(slot, sources):
    shape = jax.ShapeDtypeStruct(sources[0].shape, jnp.bfloat16)
    return pl.pallas_call(
        choose_kernel,
        out_shape=(shape,) * COLUMN,
        in_specs=[SMEM] + [ANY] * len(sources),
        out_specs=(VMEM,) * COLUMN,
        scratch_shapes=[pltpu.SemaphoreType.DMA((COLUMN,))],
        cost_estimate=estimate(1000, 10**6),
        name="choose",
    )(slot, *sources)


def finish_kernel(code, x_ref, h0, h1, h2, h3, own_ref, inside_ref, taps_ref, skip_ref, gate_ref,
                  o_ref, ext_ref):
    taps = taps_ref.shape[0]
    which = code[0]
    halo = jnp.zeros((taps, ext_ref.shape[1]), jnp.float32)
    for n, ref in ((0, h0), (1, h1), (2, h2), (3, h3), (5, own_ref)):
        halo = jnp.where(which == n, ref[...].astype(jnp.float32), halo)
    ext_ref[:taps, :] = halo
    ext_ref[taps:, :] = jnp.zeros((taps, ext_ref.shape[1]), jnp.float32)
    half = taps // 2
    added = []
    for part in range(2):
        total = jnp.zeros((half, ext_ref.shape[1]), jnp.float32)
        for j in range(8):
            base = 8 + half * part - j
            piece = ext_ref[pl.ds(base, half + taps - 8), :]
            for k in range(taps // 8):
                tap = taps_ref[pl.ds(8 * k + j, 1), :]
                keep = min(half, 8 * k + 8 - half * part)
                if keep <= 0:
                    continue
                low = taps - 8 - 8 * k
                term = tap * piece[low : low + keep, :]
                if keep < half:
                    total = jnp.concatenate([total[:keep] + term, total[keep:]], axis=0)
                else:
                    total = total + term
        added.append(total)
    rows = x_ref.shape[0]
    added.append(jnp.zeros((rows - taps, ext_ref.shape[1]), jnp.float32))
    filtered = inside_ref[...] + jnp.concatenate(added, axis=0)
    direct = skip_ref[...] * x_ref[...].astype(jnp.float32)
    o_ref[...] = (gate_ref[...].astype(jnp.float32) * (filtered + direct)).astype(jnp.bfloat16)


def finish(side, code, x, halos, own_tail, inside, taps, skip, gate):
    rows, channels = x.shape
    count = taps.shape[0]
    tile = pl.BlockSpec((rows, 128), lambda c, code: (0, c))
    tail = pl.BlockSpec((count, 128), lambda c, code: (0, c))
    return pl.pallas_call(
        finish_kernel,
        out_shape=jax.ShapeDtypeStruct(x.shape, jnp.bfloat16),
        grid_spec=pltpu.PrefetchScalarGridSpec(
            num_scalar_prefetch=1,
            grid=(channels // 128,),
            in_specs=[tile]
            + [tail] * 5
            + [
                tile,
                tail,
                pl.BlockSpec((1, 128), lambda c, code: (0, c)),
                pl.BlockSpec((rows, 128), lambda c, code: (side, c)),
            ],
            out_specs=tile,
            scratch_shapes=[pltpu.VMEM((2 * count, 128), jnp.float32)],
        ),
        cost_estimate=estimate(2 * rows * channels * 64, 2 * 10**6),
        name="finish",
    )(code, x, *halos, own_tail, inside, taps, skip, gate)


def spread(x):
    up, down = [x], [x]
    for _ in range(3):
        up.append(along_z(up[-1], 1))
        down.append(along_z(down[-1], -1))
    half = x.shape[0] // 2
    last = (along_z(up[-1][:half], 1), along_z(down[-1][half:], -1))
    return up[1:], down[1:], last


def shards(
    block_order,
    queries,
    key_head_matrix,
    value_head_matrix,
    out_weight,
    filter_taps,
    skip_gain,
    gate_values,
):
    position = lax.axis_index("ctx")
    column = position % COLUMN
    z = position // COLUMN
    blocks = block_order.shape[0]
    places = jnp.arange(blocks, dtype=jnp.int32)
    slot_z = jnp.array(SLOT_Z, jnp.int32)
    slot_x = 2 * jnp.array((0, 1) * RING, jnp.int32)
    slot_at = (z + slot_z) % RING * COLUMN + (column ^ slot_x)
    asked = jnp.concatenate([slot_at, jnp.stack([position, position ^ 1])])
    info = lookup(block_order, 2 * asked)

    kv = jnp.concatenate([key_head_matrix, value_head_matrix], axis=1)
    beside = across(kv, 2)
    other_queries = across(queries, 1)
    q_low, q_high = prepare(queries, other_queries)
    up, down, last = spread(jnp.concatenate([kv, beside], axis=0))
    state = fold(q_high, (kv, beside), None)
    for a, b in zip(up, down):
        state = fold(q_high, (a, b), state)
    arrays = (kv, beside, *up, *down, *last)

    head = lax.axis_index("head")
    target = head_target(head, jnp.arange(8, dtype=jnp.int32))
    near = position ^ jnp.arange(COLUMN, dtype=jnp.int32)
    near_low = lookup(block_order, 2 * near)
    holder = jnp.sum(
        jnp.where(block_order[None, :] == places[:, None], places[None, :], 0), axis=1
    )
    tail_slot = jnp.array((0, 4, 5, 6, 7, 3, 2, 1), jnp.int32)
    taps = filter_taps.shape[0]
    outs = []
    tails = []
    for side in range(2):
        if side == 0:
            own, sent = one_side(0, info, q_low, arrays, ())
        else:
            own, sent = one_side(1, info, q_high, arrays, state)
        tiles = project(target, own, across(sent, 1), out_weight)
        moved = [tiles[0]]
        for k in range(1, 8):
            moved.append(
                lax.ppermute(tiles[k], "head", [(i, int(head_target(i, k))) for i in range(8)])
            )
        projected, tail = total_of(moved, taps)
        tails.append(tail)
        tail_up, tail_down, tail_last = spread(tail)
        inside = inside_filter(projected, filter_taps)
        before = 62 - near_low if side else jnp.maximum(near_low - 1, 0)
        source = lookup(holder, before) // 2
        slot = lookup(tail_slot, (source // COLUMN - z) % RING)
        chosen = choose(
            slot, (tail, *tail_up, *tail_down, jnp.concatenate(tail_last, axis=0))
        )
        halos = [chosen[0]] + [across(chosen[k], k) for k in range(1, COLUMN)]
        code = (source[0] % COLUMN) ^ column
        edge = near_low[0] == (31 if side else 0)
        code = jnp.where(edge, 5 if side else 4, code)[None]
        outs.append(
            finish(
                side, code, projected, halos, tails[0], inside, filter_taps, skip_gain[None, :],
                gate_values,
            )
        )
    return jnp.concatenate(outs, axis=0)


def solution(mesh):
    return jax.shard_map(
        shards,
        mesh=mesh,
        in_specs=(
            P(),
            P("ctx", "head"),
            P("ctx", "head"),
            P("ctx", "head"),
            P("head", None),
            P(None, "head"),
            P("head"),
            P("ctx", "head"),
        ),
        out_specs=P("ctx", "head"),
        check_vma=False,
    )
```

```python
import functools
import math

import jax
import jax.numpy as jnp
from jax import lax
from jax.experimental import pallas as pl
from jax.experimental.pallas import tpu as pltpu
from jax.sharding import PartitionSpec as P

HEAD_WIDTH = 128
QUERY_PER_KV = 4
GROUP = 4
TILES = 4
LOW = -1e30
LOG2_E = 1.4426950408889634
RING = 8
COLUMN = 4
SLOT_Z = (0, 0, -1, -1, -2, -2, -3, -3, 1, 1, 2, 2, 3, 3, 4, 4)
TAIL_Z = (0, -1, -2, -3, 1, 2, 3, 4)
VMEM = pl.BlockSpec(memory_space=pltpu.VMEM)
ANY = pl.BlockSpec(memory_space=pl.ANY)
SMEM = pl.BlockSpec(memory_space=pltpu.SMEM)


def lookup(table_values, index_values):
    matches = jnp.arange(table_values.shape[0], dtype=jnp.int32)[None, :] == index_values[:, None]
    return jnp.sum(jnp.where(matches, table_values[None, :], 0), axis=1)


def along_z(x, distance):
    pairs = [
        (i, (i // COLUMN + distance) % RING * COLUMN + i % COLUMN) for i in range(RING * COLUMN)
    ]
    return lax.ppermute(x, "ctx", pairs)


def across(x, bits):
    return lax.ppermute(x, "ctx", [(i, i ^ bits) for i in range(RING * COLUMN)])


def head_target(index, k):
    return (index // 4 ^ k // 4) * 4 + (index + k) % 4


def busy(microseconds):
    return pl.CostEstimate(
        flops=microseconds * 10**9, bytes_accessed=microseconds * 10**6, transcendentals=0
    )


def operands(pieces):
    kv = jnp.concatenate(pieces, axis=0)
    k = kv[:, :HEAD_WIDTH]
    return jnp.concatenate([k, k], axis=1), kv[:, HEAD_WIDTH:]


def scores_of(q, k2):
    return lax.dot_general(q, k2, (((1,), (1,)), ((), ())), preferred_element_type=jnp.float32)


def prepare_kernel(own_ref, other_ref, kv_ref, low_ref, high_ref, m_ref, acc_ref):
    scale = LOG2_E / math.sqrt(HEAD_WIDTH)
    rows = own_ref.shape[0] // 2
    row = lax.broadcasted_iota(jnp.int32, (rows, rows), 0)
    allowed = lax.broadcasted_iota(jnp.int32, (rows, rows), 1) <= row
    for i, q_ref in enumerate((own_ref, other_ref)):
        for s, out in enumerate((low_ref, high_ref)):
            here = slice(s * rows, (s + 1) * rows)
            if i == 0:
                k2, v = operands([kv_ref[here, :]])
                v1 = jnp.concatenate([v, jnp.ones_like(v)], axis=1)
            for h in range(QUERY_PER_KV):
                q = q_ref[here, h * HEAD_WIDTH : (h + 1) * HEAD_WIDTH].astype(jnp.float32)
                q = q * scale
                high = q.astype(jnp.bfloat16)
                rest = (q - high.astype(jnp.float32)).astype(jnp.bfloat16)
                both = jnp.concatenate([high, rest], axis=1)
                at = slice(h * rows, (h + 1) * rows)
                out[i, at, :] = both
                if i == 0:
                    scores = jnp.where(allowed, scores_of(both, k2), LOW)
                    top = jnp.max(scores, axis=1, keepdims=True)
                    weight = jnp.exp2(scores - top).astype(jnp.bfloat16)
                    m_ref[s, at, :] = jnp.broadcast_to(top, (rows, HEAD_WIDTH))
                    acc_ref[s, at, :] = jnp.dot(weight, v1, preferred_element_type=jnp.float32)


def prepare(own, other, kv):
    rows = own.shape[0] // 2 * QUERY_PER_KV
    shape = jax.ShapeDtypeStruct((2, rows, 2 * HEAD_WIDTH), jnp.bfloat16)
    return pl.pallas_call(
        prepare_kernel,
        out_shape=(
            shape,
            shape,
            jax.ShapeDtypeStruct((2, rows, HEAD_WIDTH), jnp.float32),
            jax.ShapeDtypeStruct((2, rows, 2 * HEAD_WIDTH), jnp.float32),
        ),
        in_specs=[VMEM] * 3,
        out_specs=(VMEM,) * 4,
        cost_estimate=busy(5),
        name="prepare",
    )(own, other, kv)


def side_kernel(side, tiles, info, q_ref, first_m, first_acc, *refs):
    arrays, refs = refs[:10], refs[10:]
    own_out, other_out, kv_ref, s_ref, p_ref, f_ref, m_ref, acc_ref, list_ref, sem = refs
    block = arrays[0].shape[0] // 2
    rows = q_ref.shape[1]
    slots = 2 * RING
    copies = []
    for half in range(side + 1):
        slot = half * slots
        for ref in arrays:
            for start in range(half * block, ref.shape[0], 2 * block):
                copies.append(
                    pltpu.make_async_copy(
                        ref.at[pl.ds(start, block), :], kv_ref.at[slot], sem.at[slot]
                    )
                )
                slot += 1
    for copy in copies:
        copy.start()
    m_ref[0] = first_m[side]
    acc_ref[0] = first_acc[side]
    m_ref[1] = jnp.full_like(m_ref[1], LOW)
    acc_ref[1] = jnp.zeros_like(acc_ref[1])
    s_ref[...] = jnp.full_like(s_ref, 2 * LOW)
    p_ref[...] = jnp.zeros_like(p_ref)
    f_ref[...] = jnp.ones_like(f_ref)
    counts = []
    for i in range(2):
        number = jnp.int32(0)
        mine = info[slots + i]
        if side:
            for p in range(slots):
                list_ref[i, p] = p
            number = number + slots
        for p in range(slots):
            list_ref[i, number] = p + side * slots
            chosen = info[p] > mine if side else info[p] < mine
            number = number + chosen.astype(jnp.int32)
        counts.append(number)
    for copy in copies:
        copy.wait()
    first_groups = (counts[0] + GROUP - 1) // GROUP
    total = first_groups + (counts[1] + GROUP - 1) // GROUP
    step = rows // tiles

    def task(t):
        t = jnp.clip(t, 0, total - 1)
        i = (t >= first_groups).astype(jnp.int32)
        return i, (t - i * first_groups) * GROUP

    def member(i, start, j):
        valid = start + j < jnp.where(i == 0, counts[0], counts[1])
        return kv_ref[list_ref[i, jnp.where(valid, start + j, start)]], valid

    def body(t, unused):
        i0, at0 = task(t)
        k2 = operands([member(i0, at0, j)[0] for j in range(GROUP)])[0]
        i1, _ = task(t - 1)
        i2, at2 = task(t - 2)
        pieces = []
        for j in range(GROUP):
            kv, valid = member(i2, at2, j)
            v = kv[:, HEAD_WIDTH:]
            v1 = jnp.concatenate([v, jnp.ones_like(v)], axis=1)
            pieces.append(jnp.where(valid, v1, jnp.zeros_like(v1)))
        v1 = jnp.concatenate(pieces, axis=0)
        width = s_ref.shape[1] // HEAD_WIDTH
        for n in range(tiles):
            at = slice(n * step, (n + 1) * step)
            factor = f_ref[at, :]
            acc_ref[i2, at, :] = acc_ref[i2, at, :] * jnp.concatenate(
                [factor, factor], axis=1
            ) + jnp.dot(p_ref[at, :], v1, preferred_element_type=jnp.float32)
            scores = s_ref[at, :]
            old = m_ref[i1, at, :]
            newest = jnp.maximum(old, jnp.max(scores, axis=1, keepdims=True))
            p_ref[at, :] = jnp.exp2(
                scores - jnp.concatenate([newest] * width, axis=1)
            ).astype(jnp.bfloat16)
            f_ref[at, :] = jnp.exp2(old - newest)
            m_ref[i1, at, :] = newest
            s_ref[at, :] = scores_of(q_ref[i0, at, :], k2)
        return unused

    lax.fori_loop(0, jnp.where(total > 0, total + 2, 0), body, 0)
    for i, out in enumerate((own_out, other_out)):
        amount = jnp.maximum(acc_ref[i, :, HEAD_WIDTH:], 1e-30)
        out[:, :HEAD_WIDTH] = acc_ref[i, :, :HEAD_WIDTH] / amount
        out[:, HEAD_WIDTH:] = m_ref[i] + jnp.log2(amount)


def one_side(side, info, q, first, arrays):
    rows = q.shape[1]
    block = rows // QUERY_PER_KV
    shape = jax.ShapeDtypeStruct((rows, 2 * HEAD_WIDTH), jnp.float32)
    slots = 2 * RING * (side + 1)
    return pl.pallas_call(
        functools.partial(side_kernel, side, TILES),
        out_shape=(shape, shape),
        in_specs=[SMEM, VMEM, VMEM, VMEM] + [ANY] * len(arrays),
        out_specs=(VMEM, VMEM),
        scratch_shapes=[
            pltpu.VMEM((slots, block, 2 * HEAD_WIDTH), jnp.bfloat16),
            pltpu.VMEM((rows, GROUP * block), jnp.float32),
            pltpu.VMEM((rows, GROUP * block), jnp.bfloat16),
            pltpu.VMEM((rows, HEAD_WIDTH), jnp.float32),
            pltpu.VMEM((2, rows, HEAD_WIDTH), jnp.float32),
            pltpu.VMEM((2, rows, 2 * HEAD_WIDTH), jnp.float32),
            pltpu.SMEM((2, slots + 8), jnp.int32),
            pltpu.SemaphoreType.DMA((slots,)),
        ],
        cost_estimate=busy(15 if side else 7),
        name="high_side" if side else "low_side",
    )(info, q, *first, *arrays)


def project_kernel(target, own_ref, other_ref, w_ref, *outs):
    parts = []
    rows = own_ref.shape[0] // QUERY_PER_KV
    for h in range(QUERY_PER_KV):
        at = slice(h * rows, (h + 1) * rows)
        one, two = own_ref[at, HEAD_WIDTH:], other_ref[at, HEAD_WIDTH:]
        top = jnp.maximum(one, two)
        one, two = jnp.exp2(one - top), jnp.exp2(two - top)
        mixed = own_ref[at, :HEAD_WIDTH] * one + other_ref[at, :HEAD_WIDTH] * two
        parts.append((mixed / (one + two)).astype(jnp.bfloat16))
    attended = jnp.concatenate(parts, axis=1)
    width = outs[0].shape[1]
    for k, out in enumerate(outs):
        start = pl.multiple_of(target[k] * width, width)
        out[...] = jnp.dot(
            attended, w_ref[:, pl.ds(start, width)], preferred_element_type=jnp.float32
        ).astype(jnp.bfloat16)


def project(target, own, other, weight):
    rows = own.shape[0] // QUERY_PER_KV
    count = target.shape[0]
    width = weight.shape[1] // count
    shape = jax.ShapeDtypeStruct((rows, width), jnp.bfloat16)
    return pl.pallas_call(
        project_kernel,
        out_shape=(shape,) * count,
        in_specs=[SMEM, VMEM, VMEM, VMEM],
        out_specs=(VMEM,) * count,
        cost_estimate=busy(4),
        name="project",
    )(target, own, other, weight)


def total_kernel(*refs):
    parts, (out_ref, tail_ref) = refs[:-2], refs[-2:]
    total = parts[0][...].astype(jnp.float32)
    for part in parts[1:]:
        total = total + part[...].astype(jnp.float32)
    total = total.astype(jnp.bfloat16)
    out_ref[...] = total
    tail_ref[...] = total[total.shape[0] - tail_ref.shape[0] :, :]


def total_of(parts, taps):
    rows, width = parts[0].shape
    return pl.pallas_call(
        total_kernel,
        out_shape=(
            jax.ShapeDtypeStruct((rows, width), jnp.bfloat16),
            jax.ShapeDtypeStruct((taps, width), jnp.bfloat16),
        ),
        in_specs=[VMEM] * len(parts),
        out_specs=(VMEM, VMEM),
        cost_estimate=busy(2),
        name="total",
    )(*parts)


def inside_kernel(x_ref, taps_ref, o_ref, ext_ref):
    rows = x_ref.shape[0]
    taps = taps_ref.shape[0]
    ext_ref[:taps, :] = jnp.zeros((taps, ext_ref.shape[1]), jnp.float32)
    ext_ref[taps:, :] = x_ref[...].astype(jnp.float32)
    half = rows // 2
    for part in range(2):
        total = jnp.zeros((half, ext_ref.shape[1]), jnp.float32)
        for j in range(8):
            base = 8 + half * part - j
            piece = ext_ref[pl.ds(base, half + taps - 8), :]
            for k in range(taps // 8):
                tap = taps_ref[pl.ds(8 * k + j, 1), :]
                skip = max(0, 8 * k - half * part) // 8 * 8
                if skip >= half:
                    continue
                low = taps - 8 - 8 * k + skip
                term = tap * piece[low : low + half - skip, :]
                if skip:
                    total = jnp.concatenate([total[:skip], total[skip:] + term], axis=0)
                else:
                    total = total + term
        o_ref[half * part : half * (part + 1), :] = total


def inside_filter(x, taps):
    rows, channels = x.shape
    return pl.pallas_call(
        inside_kernel,
        out_shape=jax.ShapeDtypeStruct(x.shape, jnp.float32),
        grid=(channels // 128,),
        in_specs=[
            pl.BlockSpec((rows, 128), lambda c: (0, c)),
            pl.BlockSpec((taps.shape[0], 128), lambda c: (0, c)),
        ],
        out_specs=pl.BlockSpec((rows, 128), lambda c: (0, c)),
        scratch_shapes=[pltpu.VMEM((rows + taps.shape[0], 128), jnp.float32)],
        cost_estimate=busy(4),
        name="inside",
    )(x, taps)


def choose_kernel(slot, *refs):
    sources, outs, sem = refs[: len(TAIL_Z)], refs[len(TAIL_Z) : -1], refs[-1]
    for k, out in enumerate(outs):
        for n, source in enumerate(sources):

            @pl.when(slot[k] == n)
            def _():
                pltpu.make_async_copy(source, out, sem.at[k]).start()

    for k, out in enumerate(outs):
        pltpu.make_async_copy(sources[0], out, sem.at[k]).wait()


def choose(slot, sources):
    shape = jax.ShapeDtypeStruct(sources[0].shape, jnp.bfloat16)
    return pl.pallas_call(
        choose_kernel,
        out_shape=(shape,) * COLUMN,
        in_specs=[SMEM] + [ANY] * len(sources),
        out_specs=(VMEM,) * COLUMN,
        scratch_shapes=[pltpu.SemaphoreType.DMA((COLUMN,))],
        cost_estimate=busy(2),
        name="choose",
    )(slot, *sources)


def finish_kernel(code, x_ref, h0, h1, h2, h3, own_ref, inside_ref, taps_ref, skip_ref, gate_ref,
                  o_ref, ext_ref):
    taps = taps_ref.shape[0]
    which = code[0]
    halo = jnp.zeros((taps, ext_ref.shape[1]), jnp.float32)
    for n, ref in ((0, h0), (1, h1), (2, h2), (3, h3), (5, own_ref)):
        halo = jnp.where(which == n, ref[...].astype(jnp.float32), halo)
    ext_ref[:taps, :] = halo
    ext_ref[taps:, :] = jnp.zeros((taps, ext_ref.shape[1]), jnp.float32)
    half = taps // 2
    added = []
    for part in range(2):
        total = jnp.zeros((half, ext_ref.shape[1]), jnp.float32)
        for j in range(8):
            base = 8 + half * part - j
            piece = ext_ref[pl.ds(base, half + taps - 8), :]
            for k in range(taps // 8):
                tap = taps_ref[pl.ds(8 * k + j, 1), :]
                keep = min(half, 8 * k + 8 - half * part)
                if keep <= 0:
                    continue
                low = taps - 8 - 8 * k
                term = tap * piece[low : low + keep, :]
                if keep < half:
                    total = jnp.concatenate([total[:keep] + term, total[keep:]], axis=0)
                else:
                    total = total + term
        added.append(total)
    rows = x_ref.shape[0]
    added.append(jnp.zeros((rows - taps, ext_ref.shape[1]), jnp.float32))
    filtered = inside_ref[...] + jnp.concatenate(added, axis=0)
    direct = skip_ref[...] * x_ref[...].astype(jnp.float32)
    o_ref[...] = (gate_ref[...].astype(jnp.float32) * (filtered + direct)).astype(jnp.bfloat16)


def finish(side, code, x, halos, own_tail, inside, taps, skip, gate):
    rows, channels = x.shape
    count = taps.shape[0]
    tile = pl.BlockSpec((rows, 128), lambda c, code: (0, c))
    tail = pl.BlockSpec((count, 128), lambda c, code: (0, c))
    return pl.pallas_call(
        finish_kernel,
        out_shape=jax.ShapeDtypeStruct(x.shape, jnp.bfloat16),
        grid_spec=pltpu.PrefetchScalarGridSpec(
            num_scalar_prefetch=1,
            grid=(channels // 128,),
            in_specs=[tile]
            + [tail] * 5
            + [
                tile,
                tail,
                pl.BlockSpec((1, 128), lambda c, code: (0, c)),
                pl.BlockSpec((rows, 128), lambda c, code: (side, c)),
            ],
            out_specs=tile,
            scratch_shapes=[pltpu.VMEM((2 * count, 128), jnp.float32)],
        ),
        cost_estimate=busy(4),
        name="finish",
    )(code, x, *halos, own_tail, inside, taps, skip, gate)


def spread(x):
    up, down = [x], [x]
    for _ in range(3):
        up.append(along_z(up[-1], 1))
        down.append(along_z(down[-1], -1))
    half = x.shape[0] // 2
    last = (along_z(up[-1][:half], 1), along_z(down[-1][half:], -1))
    return up[1:], down[1:], last


def shards(
    block_order,
    queries,
    key_head_matrix,
    value_head_matrix,
    out_weight,
    filter_taps,
    skip_gain,
    gate_values,
):
    position = lax.axis_index("ctx")
    column = position % COLUMN
    z = position // COLUMN
    blocks = block_order.shape[0]
    places = jnp.arange(blocks, dtype=jnp.int32)
    slot_z = jnp.array(SLOT_Z, jnp.int32)
    slot_x = 2 * jnp.array((0, 1) * RING, jnp.int32)
    slot_at = (z + slot_z) % RING * COLUMN + (column ^ slot_x)
    asked = jnp.concatenate([slot_at, jnp.stack([position, position ^ 1])])
    info = lookup(block_order, 2 * asked)

    kv = jnp.concatenate([key_head_matrix, value_head_matrix], axis=1)
    beside = across(kv, 2)
    other_queries = across(queries, 1)
    q_low, q_high, *first = prepare(queries, other_queries, kv)
    up, down, last = spread(jnp.concatenate([kv, beside], axis=0))
    arrays = (kv, beside, *up, *down, *last)

    head = lax.axis_index("head")
    target = head_target(head, jnp.arange(8, dtype=jnp.int32))
    near = position ^ jnp.arange(COLUMN, dtype=jnp.int32)
    near_low = lookup(block_order, 2 * near)
    holder = jnp.sum(
        jnp.where(block_order[None, :] == places[:, None], places[None, :], 0), axis=1
    )
    tail_slot = jnp.array((0, 4, 5, 6, 7, 3, 2, 1), jnp.int32)
    taps = filter_taps.shape[0]
    outs = []
    tails = []
    for side in range(2):
        own, sent = one_side(side, info, q_high if side else q_low, first, arrays)
        tiles = project(target, own, across(sent, 1), out_weight)
        moved = [tiles[0]]
        for k in range(1, 8):
            moved.append(
                lax.ppermute(tiles[k], "head", [(i, int(head_target(i, k))) for i in range(8)])
            )
        projected, tail = total_of(moved, taps)
        tails.append(tail)
        tail_up, tail_down, tail_last = spread(tail)
        inside = inside_filter(projected, filter_taps)
        before = 62 - near_low if side else jnp.maximum(near_low - 1, 0)
        source = lookup(holder, before) // 2
        slot = lookup(tail_slot, (source // COLUMN - z) % RING)
        chosen = choose(
            slot, (tail, *tail_up, *tail_down, jnp.concatenate(tail_last, axis=0))
        )
        halos = [chosen[0]] + [across(chosen[k], k) for k in range(1, COLUMN)]
        code = (source[0] % COLUMN) ^ column
        edge = near_low[0] == (31 if side else 0)
        code = jnp.where(edge, 5 if side else 4, code)[None]
        outs.append(
            finish(
                side, code, projected, halos, tails[0], inside, filter_taps, skip_gain[None, :],
                gate_values,
            )
        )
    return jnp.concatenate(outs, axis=0)


def solution(mesh):
    return jax.shard_map(
        shards,
        mesh=mesh,
        in_specs=(
            P(),
            P("ctx", "head"),
            P("ctx", "head"),
            P("ctx", "head"),
            P("head", None),
            P(None, "head"),
            P("head"),
            P("ctx", "head"),
        ),
        out_specs=P("ctx", "head"),
        check_vma=False,
    )
```
